32 devices in a mesh: ctx: 4 (over z), exp: 4 (over y, x), rep: 2 (over core).
Axes of the slice: x: 2, y: 2, z: 4, core: 2. Of those that a mesh axis runs over, the one named last changes fastest.
Arguments:
- acts: bfloat16 [512, 2048], P(('ctx', 'exp'), 'rep'), may hold values from -6 to 6
- grad_out: bfloat16 [512, 2048], P(('ctx', 'exp'), 'rep'), may hold values from -0.59765625 to 0.59765625
- experts_idx: int32 [512, 8], P(('ctx', 'exp')), may hold values from 0 to 15, all different within a row; in each aligned block of 32 rows (0 to 31, 32 to 63, ...) at most 24 rows name the same one
- gate_prob: bfloat16 [512, 8], P(('ctx', 'exp')), may hold values from 0.049804688 to 1
- w_gate: bfloat16 [16, 768, 2048], P(('ctx', 'exp'), 'rep'), may hold values from -0.125 to 0.125
- w_up: bfloat16 [16, 768, 2048], P(('ctx', 'exp'), 'rep'), may hold values from -0.125 to 0.125
- w_down: bfloat16 [16, 768, 2048], P(('ctx', 'exp'), 'rep'), may hold values from -0.21875 to 0.21875
Outputs:
- acts_grad: bfloat16 [512, 2048], P(('ctx', 'exp'), 'rep')
- gate_grad_tok: bfloat16 [512, 8], P(('ctx', 'exp'))
- w_gate_grad: bfloat16 [16, 768, 2048], P(('ctx', 'exp'), 'rep')
- w_up_grad: bfloat16 [16, 768, 2048], P(('ctx', 'exp'), 'rep')
- w_down_grad: bfloat16 [16, 768, 2048], P(('ctx', 'exp'), 'rep')
The draws below stay inside these ranges and needn't reach their ends.
Inputs may be any that keep to these rules, and one draw needn't show every extreme that they name: `experts_idx`: each row names 8 different experts. Within the rows of one index of ctx+exp (32 aligned rows), no expert is named by more than 24 rows, a bound that some block reaches.
All inputs are finite; a program needn't handle non-finite values.
Results may differ from the reference program's by a relative error of at most 0.012.
Values may be sent and summed in bfloat16 or wider, within the bound.
A program may use at most 64 MiB of HBM per device.

```python
import math
import jax
import jax.numpy as jnp
import numpy as np
from jax import lax

D = 2048
FF = 768
TOP = 8
TOK_DEV = 32
EXPERTS = 16
TOKENS = 512
CAP = 24
N_CTX = 4
N_EXP = 4
N_REP = 2


def level_of(own_key, shape, split, smallest, top_value):
    loudness = 1.0
    for position, blocks in split:
        heights = jax.random.uniform(jax.random.fold_in(jax.random.fold_in(own_key, 6), position), (blocks,), jnp.float32, smallest / len(split), top_value / len(split))
        loudness = loudness * jnp.repeat(jnp.exp(heights), shape[position] // blocks).reshape((-1,) + (1,) * (len(shape) - 1 - position))
    return loudness


def assign_block(key, own, number, rows, number_of, top, reach, skew):
    ranking = jax.random.permutation(key, number_of)
    heavy_load, common = shares(number_of, rows * top, reach, skew, True), shares(number_of, rows * top, reach, skew, False)
    places = jnp.arange(number_of)

    def named(lengths, turn):
        used = int((lengths > 0).sum())
        fixed = max(1, used // 4)
        passed = fixed + (places - fixed + turn * (used - fixed)) % max(1, number_of - fixed)
        return jnp.zeros((number_of,), jnp.int32).at[ranking[jnp.where(places < fixed, places, passed)]].set(jnp.asarray(lengths, jnp.int32))

    lengths = jnp.where(number % 4 == 0, named(heavy_load, number // 4), named(common, number - number // 4 - 1))
    mixed = jax.random.permutation(jax.random.fold_in(own, 3), number_of)
    donor, receiver = mixed[0:number_of // 2 * 2:2], mixed[1:number_of // 2 * 2:2]
    slack = jnp.minimum(lengths[donor] - 1, reach - lengths[receiver]) // 2
    slack = jnp.where((donor == ranking[0]) | (receiver == ranking[0]) | (lengths[receiver] == 0), 0, jnp.maximum(slack, 0))
    passed = jax.random.randint(jax.random.fold_in(own, 4), (number_of // 2,), 0, 1 << 20) % (slack + 1)
    lengths = lengths.at[donor].add(-passed).at[receiver].add(passed)
    items = jnp.searchsorted(jnp.cumsum(lengths), jnp.arange(rows * top), side="right").astype(jnp.int32)
    grid = items.reshape(top, rows).T
    grid = grid[jax.random.permutation(jax.random.fold_in(own, 1), rows)]
    turn = jax.random.randint(jax.random.fold_in(own, 2), (rows, 1), 0, top)
    return jnp.take_along_axis(grid, (jnp.arange(top)[None, :] + turn) % top, axis=1)


def shares(number_of, total, limit, lean, full):
    weights = [(1 << 20) // math.isqrt(standing ** lean) + 1 for standing in range(1, number_of + 1)]
    largest = limit if full else min(limit, max(-(-total // number_of), total * weights[0] // sum(weights)))
    least = 1 if total - largest >= number_of - 1 else 0
    given, spare = [largest] + [least] * (number_of - 1), total - largest - least * (number_of - 1)
    while spare > 0:
        movable = [i for i in range(1, number_of) if given[i] < largest] or [i for i in range(1, number_of) if given[i] < limit]
        pool, budget = sum([weights[i] for i in movable]), spare
        for i in movable:
            more = min(limit - given[i], max(1, budget * weights[i] // pool), spare)
            given[i] = given[i] + more
            spare = spare - more
    return np.array(given)


def gaussian(key, shape, deviation, reach, shards=(), kind=jnp.bfloat16):
    factor_of = level_of(key, shape, shards, -0.22, 0.18) if shards else 1.0
    array = jax.random.normal(key, shape, jnp.float32) * deviation * factor_of
    return jnp.minimum(jnp.maximum(array, -reach), reach).astype(kind)


def setup_inputs(seed: int = 0) -> dict:
    keys = jax.random.split(jax.random.key(seed), 8)
    acts = gaussian(keys[0], (TOKENS, D), 1.0, 6.0, ((0, 16), (1, 2)))
    grad_out = gaussian(keys[1], (TOKENS, D), 0.1, 0.59765625, ((0, 16), (1, 2)))
    experts_idx_keys = jax.random.split(jax.random.fold_in(keys[2], 1), TOKENS // TOK_DEV)
    experts_idx_turns = jax.random.permutation(jax.random.fold_in(keys[2], 3), TOKENS // TOK_DEV)
    experts_idx = jax.vmap(lambda own, number: assign_block(jax.random.fold_in(keys[2], 2), own, number, TOK_DEV, EXPERTS, TOP, CAP, 2))(experts_idx_keys, experts_idx_turns).reshape((TOKENS, TOP))
    gate_prob = jnp.clip(jnp.exp(math.log(1.0) - 2.9996462 * jax.random.uniform(keys[3], (TOKENS, TOP), jnp.float32) ** level_of(keys[3], (TOKENS, TOP), ((0, 16),), -0.2, 0.2)), 0.049804688, 1.0).astype(jnp.bfloat16)
    w_gate = gaussian(keys[4], (EXPERTS, FF, D), D ** -0.5, 0.125, ((0, 16), (1, 2)))
    w_up = gaussian(keys[5], (EXPERTS, FF, D), D ** -0.5, 0.125, ((0, 16), (1, 2)))
    w_down = gaussian(keys[6], (EXPERTS, FF, D), FF ** -0.5, 0.21875, ((0, 16), (1, 2)))
    return {"acts": acts, "grad_out": grad_out, "experts_idx": experts_idx, "gate_prob": gate_prob, "w_gate": w_gate, "w_up": w_up, "w_down": w_down}


def expert_pass(rows_acts, rows_grad, rows_gate, gate_w, up_w, down_w):
    pre_gate = jnp.dot(rows_acts, gate_w.T, preferred_element_type=jnp.float32)
    pre_up = jnp.dot(rows_acts, up_w.T, preferred_element_type=jnp.float32)
    sigma = jax.nn.sigmoid(pre_gate)
    swish = pre_gate * sigma
    hidden = (swish * pre_up).astype(jnp.bfloat16)
    expert_out = jnp.dot(hidden, down_w, preferred_element_type=jnp.float32)
    gate_total = jnp.sum(expert_out * rows_grad.astype(jnp.float32), axis=1).astype(jnp.bfloat16)
    scaled_grad = (rows_gate.astype(jnp.float32)[:, None] * rows_grad.astype(jnp.float32)).astype(jnp.bfloat16)
    hidden_grad = jnp.dot(scaled_grad, down_w.T, preferred_element_type=jnp.float32)
    grad_gate_pre = (hidden_grad * pre_up * sigma * (1.0 + pre_gate * (1.0 - sigma))).astype(jnp.bfloat16)
    grad_up_pre = (hidden_grad * swish).astype(jnp.bfloat16)
    down_grad = jnp.dot(hidden.T, scaled_grad, preferred_element_type=jnp.float32).astype(jnp.bfloat16)
    gate_grad = jnp.dot(grad_gate_pre.T, rows_acts, preferred_element_type=jnp.float32).astype(jnp.bfloat16)
    up_grad = jnp.dot(grad_up_pre.T, rows_acts, preferred_element_type=jnp.float32).astype(jnp.bfloat16)
    share = FF // N_REP
    row_terms = jnp.zeros((rows_acts.shape[0], D), jnp.float32)
    for piece in range(N_REP):
        lower = piece * share
        upper = lower + share
        partial_sum = jnp.dot(grad_gate_pre[:, lower:upper], gate_w[lower:upper], preferred_element_type=jnp.float32)
        partial_sum = partial_sum + jnp.dot(grad_up_pre[:, lower:upper], up_w[lower:upper], preferred_element_type=jnp.float32)
        rounded = lax.optimization_barrier(partial_sum.astype(jnp.bfloat16))
        row_terms = row_terms + rounded.astype(jnp.float32)
    return row_terms.astype(jnp.bfloat16), gate_total, gate_grad, up_grad, down_grad


def reference(acts, grad_out, experts_idx, gate_prob, w_gate, w_up, w_down):
    tokens_all = acts.shape[0]
    rows_most = CAP * N_CTX * N_EXP
    acts_pad = jnp.concatenate([acts, jnp.zeros((1, D), jnp.bfloat16)], axis=0)
    grad_pad = jnp.concatenate([grad_out, jnp.zeros((1, D), jnp.bfloat16)], axis=0)

    def visit(carry, inputs):
        expert_id, gate_w, up_w, down_w = inputs
        match = experts_idx == expert_id
        routed = jnp.any(match, axis=1)
        token_gate = jnp.sum(jnp.where(match, gate_prob.astype(jnp.float32), 0.0), axis=1).astype(jnp.bfloat16)
        gate_pad = jnp.concatenate([token_gate, jnp.zeros((1,), jnp.bfloat16)], axis=0)
        rows = jnp.nonzero(routed, size=rows_most, fill_value=tokens_all)[0].astype(jnp.int32)
        row_terms, gate_total, gate_grad, up_grad, down_grad = expert_pass(
            acts_pad[rows], grad_pad[rows], gate_pad[rows], gate_w, up_w, down_w)
        acts_acc = carry[0].at[rows].add(row_terms.astype(jnp.float32), mode="drop")
        gate_row = jnp.zeros((tokens_all + 1,), jnp.float32).at[rows].set(gate_total.astype(jnp.float32))
        gate_acc = carry[1] + jnp.where(match, gate_row[:tokens_all, None], 0.0)
        return (acts_acc, gate_acc), (gate_grad, up_grad, down_grad)

    start = (jnp.zeros((tokens_all, D), jnp.float32), jnp.zeros((tokens_all, TOP), jnp.float32))
    (acts_acc, gate_acc), (gate_grads, up_grads, down_grads) = lax.scan(
        visit, start, (jnp.arange(EXPERTS, dtype=jnp.int32), w_gate, w_up, w_down))
    return acts_acc.astype(jnp.bfloat16), gate_acc.astype(jnp.bfloat16), gate_grads, up_grads, down_grads
```

```python
import functools
import heapq

import jax
import jax.numpy as jnp
from jax import lax
from jax.experimental import pallas as pl
from jax.experimental.pallas import tpu as pltpu
from jax.sharding import PartitionSpec as P

MESH = pl.DeviceIdType.MESH
LANES = 128
CONTRACT_LAST = (((1,), (1,)), ((), ()))
CONTRACT_FIRST = (((0,), (0,)), ((), ()))


def diag_planes(z, planes):
    low = z - (2 * z >= planes)
    return (low, low + 1)


def forwards(z, planes, array, source, rel):
    out = []
    if rel == 0:
        out += [("x", z, 1), ("y", z, 2)]
        if source <= z < planes - 1:
            out.append(("up", z + 1, 0))
        if source >= z > 0:
            out.append(("down", z - 1, 0))
    elif rel == 1:
        if array == 1 and source in diag_planes(z, planes):
            out.append(("y", z, 3))
    elif rel == 2:
        if array == 0 and source in diag_planes(z, planes):
            out.append(("x", z, 3))
    else:
        if source <= z < planes - 1 and source not in diag_planes(z + 1, planes):
            out.append(("up", z + 1, 3))
        if source >= z > 0 and source not in diag_planes(z - 1, planes):
            out.append(("down", z - 1, 3))
    return out


def arrival_order(planes):
    wire, hop = 1.4, 1.6
    order = [[] for _ in range(planes)]
    free = {}
    events = []
    count = 0
    for z in range(planes):
        for array in range(2):
            events.append((0.0, count, z, array, z, 0))
            count += 1
    heapq.heapify(events)
    while events:
        now, _, z, array, source, rel = heapq.heappop(events)
        order[z].append((array, source, rel))
        for link, to, rel_there in forwards(z, planes, array, source, rel):
            begin = max(now, free.get((z, link), 0.0))
            free[(z, link)] = begin + wire
            heapq.heappush(events, (begin + wire + hop, count, to, array, source, rel_there))
            count += 1
    return order


def at_xor(e, rel):
    x, y = e % 2, e // 2
    dx, dy = rel % 2, rel // 2
    new_x = x if dx == 0 else 1 - x
    new_y = y if dy == 0 else 1 - y
    return new_y * 2 + new_x


def position():
    return lax.axis_index("ctx"), lax.axis_index("exp"), lax.axis_index("rep")


def greet_all(planes):
    z, e, r = position()
    barrier = pltpu.get_barrier_semaphore()
    total = 0
    for dz in range(planes):
        for rel in range(4):
            for dr in range(2):
                if dz == 0 and rel == 0 and dr == 0:
                    continue
                pl.semaphore_signal(
                    barrier,
                    inc=1,
                    device_id={
                        "ctx": lax.rem(z + dz, planes),
                        "exp": at_xor(e, rel),
                        "rep": r if dr == 0 else 1 - r,
                    },
                    device_id_type=MESH,
                )
                total += 1
    pl.semaphore_wait(barrier, total)


LINKS = ("x", "y", "up", "down", "core")


def gather_kernel(
    planes, acts, grad, gates, acts_all, grad_all, gates_all,
    send_sem, recv_sem, core_sem, gate_send, gate_recv, local_sem,
):
    z, e, r = position()
    rows, width = acts.shape
    chips = planes * 4
    greet_all(planes)

    me = z * 4 + e
    gate_copies = []
    for j in range(1, chips):
        to = lax.rem(me + j, chips)
        gate_copies.append(
            pltpu.make_async_remote_copy(
                src_ref=gates.at[to],
                dst_ref=gates_all.at[me],
                send_sem=gate_send.at[j],
                recv_sem=gate_recv.at[j],
                device_id={"ctx": to // 4, "exp": to % 4, "rep": r},
                device_id_type=MESH,
            )
        )
    inputs, outputs = (acts, grad), (acts_all, grad_all)
    mine = pl.ds(pl.multiple_of(me * rows, rows), rows)
    cols = pl.ds(pl.multiple_of(r * width, width), width)
    other_cols = pl.ds(pl.multiple_of((1 - r) * width, width), width)
    local = [
        pltpu.make_async_copy(inputs[a], outputs[a].at[mine, cols], local_sem.at[a]) for a in range(2)
    ]
    local.append(pltpu.make_async_copy(gates.at[me], gates_all.at[me], local_sem.at[2]))

    def chunk(array, source, rel, columns):
        first = pl.multiple_of((source * 4 + at_xor(e, rel)) * rows, rows)
        return outputs[array].at[pl.ds(first, rows), columns]

    def send(zi, array, source, rel, link, rel_there):
        target = {
            "x": {"ctx": z, "exp": at_xor(e, 1), "rep": r},
            "y": {"ctx": z, "exp": at_xor(e, 2), "rep": r},
            "up": {"ctx": z + 1, "exp": e, "rep": r},
            "down": {"ctx": z - 1, "exp": e, "rep": r},
            "core": {"ctx": z, "exp": e, "rep": 1 - r},
        }[link]
        place = chunk(array, source, rel, cols)
        own = source == zi and rel == 0
        sem = core_sem if link == "core" else recv_sem
        return pltpu.make_async_remote_copy(
            src_ref=inputs[array] if own else place,
            dst_ref=place,
            send_sem=send_sem.at[LINKS.index(link), array, source, rel],
            recv_sem=sem.at[array, source, rel_there],
            device_id=target,
            device_id_type=MESH,
        )

    def arrived(ref, sem):
        pltpu.make_async_copy(ref, ref, sem).wait()

    order = arrival_order(planes)
    for zi in range(planes):

        @pl.when(z == zi)
        def _():
            sent = []
            gates_out = False
            for array, source, rel in order[zi]:
                own = source == zi and rel == 0
                if not own:
                    if not gates_out:
                        for copy in gate_copies:
                            copy.start()
                        for copy in local:
                            copy.start()
                        gates_out = True
                    arrived(chunk(array, source, rel, cols), recv_sem.at[array, source, rel])
                steps = forwards(zi, planes, array, source, rel) + [("core", zi, rel)]
                for link, _, rel_there in steps:
                    copy = send(zi, array, source, rel, link, rel_there)
                    copy.start()
                    sent.append(copy)
            for copy in sent:
                copy.wait_send()

    for copy in local:
        copy.wait()
    for j in range(1, chips):
        gate_copies[j - 1].wait_send()
        arrived(gates_all.at[lax.rem(me + chips - j, chips)], gate_recv.at[j])
    for array in range(2):
        for source in range(planes):
            for rel in range(4):
                arrived(chunk(array, source, rel, other_cols), core_sem.at[array, source, rel])


def expert_kernel(
    acts, grad, gates, w_gate, w_up, w_down,
    terms, gate_part, gate_grad, up_grad, down_grad,
    gg_buf, gu_buf, gh_buf,
):
    tokens, depth = acts.shape
    hidden_here = w_gate.shape[0]
    step = LANES
    partial = jnp.zeros((tokens, LANES), jnp.float32)
    gate_col = gates[...]
    for first in range(0, hidden_here, step):
        part = pl.ds(first, step)
        pre_gate = lax.dot_general(acts[...], w_gate[part, :], CONTRACT_LAST, preferred_element_type=jnp.float32)
        pre_up = lax.dot_general(acts[...], w_up[part, :], CONTRACT_LAST, preferred_element_type=jnp.float32)
        raw = lax.dot_general(grad[...], w_down[part, :], CONTRACT_LAST, preferred_element_type=jnp.float32)
        sigma = jax.nn.sigmoid(pre_gate)
        swish = pre_gate * sigma
        hidden = (swish * pre_up).astype(jnp.bfloat16).astype(jnp.float32)
        partial = partial + hidden * raw
        hidden_grad = raw * gate_col
        gg_buf[:, part] = (
            hidden_grad * pre_up * sigma * (1.0 + pre_gate * (1.0 - sigma))
        ).astype(jnp.bfloat16)
        gu_buf[:, part] = (hidden_grad * swish).astype(jnp.bfloat16)
        gh_buf[:, part] = (hidden * gate_col).astype(jnp.bfloat16)
    flat = jnp.sum(jnp.transpose(partial), axis=0, keepdims=True)
    for block in range(gate_part.shape[0]):
        gate_part[block] = flat[:, block * LANES : (block + 1) * LANES]
    wide = 512
    for first in range(0, depth, wide):
        part = pl.ds(first, wide)
        terms[:, part] = (
            jnp.dot(gg_buf[...], w_gate[:, part], preferred_element_type=jnp.float32)
            + jnp.dot(gu_buf[...], w_up[:, part], preferred_element_type=jnp.float32)
        ).astype(jnp.bfloat16)
        gate_grad[:, part] = lax.dot_general(
            gg_buf[...], acts[:, part], CONTRACT_FIRST, preferred_element_type=jnp.float32
        ).astype(jnp.bfloat16)
        up_grad[:, part] = lax.dot_general(
            gu_buf[...], acts[:, part], CONTRACT_FIRST, preferred_element_type=jnp.float32
        ).astype(jnp.bfloat16)
        down_grad[:, part] = lax.dot_general(
            gh_buf[...], grad[:, part], CONTRACT_FIRST, preferred_element_type=jnp.float32
        ).astype(jnp.bfloat16)


def scatter_kernel(
    planes, terms, gate_part, acts_grad, gate_in,
    core_buf, sum_buf, xy_buf, col_buf, z_buf,
    core_send, core_recv, xy_send, xy_recv, z_send, z_recv, g_send, g_recv, local_sem,
):
    z, e, r = position()
    rows, width = acts_grad.shape
    plane_rows = 4 * rows
    greet_all(planes)
    me = z * 4 + e
    cols = pl.ds(pl.multiple_of(r * width, width), width)
    other_cols = pl.ds(pl.multiple_of((1 - r) * width, width), width)
    order = list(range(1, planes)) + [0]

    core_copies = {}
    for k in order:
        place = pl.ds(pl.multiple_of(lax.rem(z + k, planes) * plane_rows, plane_rows), plane_rows)
        core_copies[k] = pltpu.make_async_remote_copy(
            src_ref=terms.at[place, other_cols],
            dst_ref=core_buf.at[place],
            send_sem=core_send.at[k],
            recv_sem=core_recv.at[k],
            device_id={"ctx": z, "exp": e, "rep": 1 - r},
            device_id_type=MESH,
        )
        core_copies[k].start()

    gate_copies = []
    for k in range(planes):
        to_z = lax.rem(z + k, planes)
        for rel in range(4):
            for dr in range(2):
                if k == 0 and rel == 0 and dr == 0:
                    continue
                gate_copies.append(
                    pltpu.make_async_remote_copy(
                        src_ref=gate_part.at[to_z],
                        dst_ref=gate_in.at[r * planes * 4 + me],
                        send_sem=g_send.at[k, rel, dr],
                        recv_sem=g_recv.at[k, rel, dr],
                        device_id={
                            "ctx": to_z,
                            "exp": at_xor(e, rel),
                            "rep": r if dr == 0 else 1 - r,
                        },
                        device_id_type=MESH,
                    )
                )
    own_gate = pltpu.make_async_copy(gate_part.at[z], gate_in.at[r * planes * 4 + me], local_sem)
    own_gate.start()

    xy_copies = {}
    for k in order:
        zz = lax.rem(z + k, planes)
        core_copies[k].wait_recv()
        for rel in (3, 1, 2, 0):
            block = pl.ds(pl.multiple_of((zz * 4 + at_xor(e, rel)) * rows, rows), rows)
            sum_buf[block, :] = (
                terms[block, cols].astype(jnp.float32) + core_buf[block, :].astype(jnp.float32)
            ).astype(jnp.bfloat16)
            if rel == 0:
                continue
            xy_copies[k, rel] = pltpu.make_async_remote_copy(
                src_ref=sum_buf.at[block],
                dst_ref=xy_buf.at[k, rel],
                send_sem=xy_send.at[k, rel],
                recv_sem=xy_recv.at[k, rel],
                device_id={"ctx": z, "exp": at_xor(e, rel), "rep": r},
                device_id_type=MESH,
            )
            xy_copies[k, rel].start()
    for copy in gate_copies:
        copy.start()

    z_copies = {}
    for k in order:
        zz = lax.rem(z + k, planes)
        block = pl.ds(pl.multiple_of((zz * 4 + e) * rows, rows), rows)
        total = sum_buf[block, :].astype(jnp.float32)
        for rel in (1, 2, 3):
            xy_copies[k, rel].wait_recv()
            total = total + xy_buf[k, rel].astype(jnp.float32)
        if k == 0:
            for kk in range(1, planes):
                z_copies[kk].wait_recv()
                total = total + z_buf[kk].astype(jnp.float32)
            acts_grad[...] = total.astype(jnp.bfloat16)
            continue
        col_buf[k] = total.astype(jnp.bfloat16)
        z_copies[k] = pltpu.make_async_remote_copy(
            src_ref=col_buf.at[k],
            dst_ref=z_buf.at[k],
            send_sem=z_send.at[k],
            recv_sem=z_recv.at[k],
            device_id={"ctx": zz, "exp": e, "rep": r},
            device_id_type=MESH,
        )
        z_copies[k].start()

    own_gate.wait()
    for copies in (core_copies, xy_copies, z_copies):
        for copy in copies.values():
            copy.wait_send()
    for copy in gate_copies:
        copy.wait_send()
    for k in range(planes):
        from_z = lax.rem(z + planes - k, planes)
        for rel in range(4):
            for dr in range(2):
                if k == 0 and rel == 0 and dr == 0:
                    continue
                from_r = r if dr == 0 else 1 - r
                place = gate_in.at[from_r * planes * 4 + from_z * 4 + at_xor(e, rel)]
                pltpu.make_async_copy(place, place, g_recv.at[k, rel, dr]).wait()


def dense_body(planes, acts, grad_out, experts_idx, gate_prob, w_gate, w_up, w_down):
    rows, width = acts.shape
    top = experts_idx.shape[1]
    chips = planes * 4
    tokens = chips * rows
    depth = 2 * width
    hidden_here = w_gate.shape[1]
    dma, vmem = pltpu.SemaphoreType.DMA, pl.BlockSpec(memory_space=pltpu.VMEM)
    bf16, f32 = jnp.bfloat16, jnp.float32

    labels = jnp.arange(chips, dtype=jnp.int32)
    picked = experts_idx.T[:, None, :] == labels[None, :, None]
    gates = jnp.sum(jnp.where(picked, gate_prob.astype(f32).T[:, None, :], 0.0), axis=0)
    gates = jnp.pad(gates, ((0, 0), (0, LANES - rows)))[:, None, :]

    acts_all, grad_all, gates_all = pl.pallas_call(
        functools.partial(gather_kernel, planes),
        out_shape=(
            jax.ShapeDtypeStruct((tokens, depth), bf16),
            jax.ShapeDtypeStruct((tokens, depth), bf16),
            jax.ShapeDtypeStruct((chips, 1, LANES), f32),
        ),
        in_specs=[vmem] * 3,
        out_specs=[vmem] * 3,
        scratch_shapes=[
            dma((len(LINKS), 2, planes, 4)),
            dma((2, planes, 4)),
            dma((2, planes, 4)),
            dma((chips,)),
            dma((chips,)),
            dma((3,)),
        ],
        compiler_params=pltpu.CompilerParams(collective_id=0, has_side_effects=True),
        name="gather",
    )(acts, grad_out, gates)

    gate_col = gates_all[:, 0, :rows].reshape(tokens, 1)
    wide = jax.ShapeDtypeStruct((hidden_here, depth), bf16)
    terms, gate_part, gate_grad, up_grad, down_grad = pl.pallas_call(
        expert_kernel,
        out_shape=(
            jax.ShapeDtypeStruct((tokens, depth), bf16),
            jax.ShapeDtypeStruct((tokens // LANES, 1, LANES), f32),
            wide, wide, wide,
        ),
        in_specs=[vmem] * 6,
        out_specs=[vmem] * 5,
        scratch_shapes=[pltpu.VMEM((tokens, hidden_here), bf16)] * 3,
        compiler_params=pltpu.CompilerParams(vmem_limit_bytes=48 << 20),
        name="expert",
    )(acts_all, grad_all, gate_col, w_gate[0], w_up[0], w_down[0])

    acts_grad, gate_in = pl.pallas_call(
        functools.partial(scatter_kernel, planes),
        out_shape=(
            jax.ShapeDtypeStruct((rows, width), bf16),
            jax.ShapeDtypeStruct((2 * chips, 1, LANES), f32),
        ),
        in_specs=[vmem] * 2,
        out_specs=[vmem] * 2,
        scratch_shapes=[
            pltpu.VMEM((tokens, width), bf16),
            pltpu.VMEM((tokens, width), bf16),
            pltpu.VMEM((planes, 4, rows, width), bf16),
            pltpu.VMEM((planes, rows, width), bf16),
            pltpu.VMEM((planes, rows, width), bf16),
            dma((planes,)),
            dma((planes,)),
            dma((planes, 4)),
            dma((planes, 4)),
            dma((planes,)),
            dma((planes,)),
            dma((planes, 4, 2)),
            dma((planes, 4, 2)),
            dma,
        ],
        compiler_params=pltpu.CompilerParams(collective_id=1, has_side_effects=True),
        name="scatter",
    )(terms, gate_part)

    both = (gate_in[:chips, 0, :] + gate_in[chips:, 0, :]).astype(bf16).astype(f32)
    both = lax.dynamic_slice(both, (0, lax.axis_index("exp") * rows), (chips, rows))
    gate_grad_tok = jnp.sum(jnp.where(picked, both[None], 0.0), axis=1).T.astype(bf16)
    return acts_grad, gate_grad_tok, gate_grad[None], up_grad[None], down_grad[None]


def slot_tables(experts_idx, expert_count, capacity):
    tokens_here, top_count = experts_idx.shape
    labels = jnp.arange(expert_count, dtype=jnp.int32)
    picked = (experts_idx[:, :, None] == labels[None, None, :]).astype(jnp.int32)
    flat_pick = picked.reshape(tokens_here * top_count, expert_count)
    earlier = jnp.cumsum(flat_pick, axis=0) - flat_pick
    slot_number = jnp.sum(flat_pick * (labels[None, :] * capacity + earlier), axis=1)
    slot_labels = jnp.arange(expert_count * capacity, dtype=jnp.int32)
    select = (slot_number[None, :] == slot_labels[:, None]).astype(jnp.bfloat16)
    placing = jnp.sum(select.reshape(expert_count * capacity, tokens_here, top_count), axis=2)
    return (select, placing)


def sparse_body(acts, grad_out, experts_idx, gate_prob, w_gate, w_up, w_down):
    tokens_here, top_count = experts_idx.shape
    expert_count = lax.axis_size(("ctx", "exp"))
    capacity = min(tokens_here, 3 * tokens_here * top_count // (2 * expert_count))
    select, placing = slot_tables(experts_idx, expert_count, capacity)
    slot_gate = jnp.dot(select, gate_prob.reshape(-1), preferred_element_type=jnp.float32).astype(
        jnp.bfloat16
    )
    send_acts = jnp.dot(placing, acts, preferred_element_type=jnp.float32).astype(jnp.bfloat16)
    send_grad = jnp.dot(placing, grad_out, preferred_element_type=jnp.float32).astype(jnp.bfloat16)
    part_acts, part_grad, rows_gate = (
        lax.all_to_all(send_acts, ("ctx", "exp"), split_axis=0, concat_axis=0, tiled=True),
        lax.all_to_all(send_grad, ("ctx", "exp"), split_axis=0, concat_axis=0, tiled=True),
        lax.all_to_all(slot_gate, ("ctx", "exp"), split_axis=0, concat_axis=0, tiled=True),
    )
    rows_acts, rows_grad = (
        lax.all_gather(part_acts, "rep", axis=1, tiled=True),
        lax.all_gather(part_grad, "rep", axis=1, tiled=True),
    )
    gate_w = w_gate[0]
    up_w = w_up[0]
    down_w = w_down[0]
    contract_last = (((1,), (1,)), ((), ()))
    contract_first = (((0,), (0,)), ((), ()))
    pre_gate = lax.dot_general(rows_acts, gate_w, contract_last, preferred_element_type=jnp.float32)
    pre_up = lax.dot_general(rows_acts, up_w, contract_last, preferred_element_type=jnp.float32)
    sigma = jax.nn.sigmoid(pre_gate)
    swish = pre_gate * sigma
    hidden = (swish * pre_up).astype(jnp.bfloat16)
    expert_out = jnp.dot(hidden, down_w, preferred_element_type=jnp.float32)
    gate_part = jnp.sum(expert_out * rows_grad.astype(jnp.float32), axis=1)
    scaled_grad = (rows_gate.astype(jnp.float32)[:, None] * rows_grad.astype(jnp.float32)).astype(
        jnp.bfloat16
    )
    hidden_grad = lax.dot_general(
        scaled_grad, down_w, contract_last, preferred_element_type=jnp.float32
    )
    grad_gate_pre = (hidden_grad * pre_up * sigma * (1.0 + pre_gate * (1.0 - sigma))).astype(
        jnp.bfloat16
    )
    grad_up_pre = (hidden_grad * swish).astype(jnp.bfloat16)
    down_grad = lax.dot_general(
        hidden, scaled_grad, contract_first, preferred_element_type=jnp.float32
    ).astype(jnp.bfloat16)
    gate_grad = lax.dot_general(
        grad_gate_pre, rows_acts, contract_first, preferred_element_type=jnp.float32
    ).astype(jnp.bfloat16)
    up_grad = lax.dot_general(
        grad_up_pre, rows_acts, contract_first, preferred_element_type=jnp.float32
    ).astype(jnp.bfloat16)
    row_terms = jnp.dot(grad_gate_pre, gate_w, preferred_element_type=jnp.float32)
    row_terms = row_terms + jnp.dot(grad_up_pre, up_w, preferred_element_type=jnp.float32)
    row_share = lax.psum_scatter(
        row_terms.astype(jnp.bfloat16), "rep", scatter_dimension=1, tiled=True
    )
    gate_total = lax.psum(gate_part, "rep").astype(jnp.bfloat16)
    back_share, back_gate = (
        lax.all_to_all(row_share, ("ctx", "exp"), split_axis=0, concat_axis=0, tiled=True),
        lax.all_to_all(gate_total, ("ctx", "exp"), split_axis=0, concat_axis=0, tiled=True),
    )
    acts_grad = lax.dot_general(
        placing, back_share, contract_first, preferred_element_type=jnp.float32
    ).astype(jnp.bfloat16)
    gate_flat = lax.dot_general(
        select, back_gate, contract_first, preferred_element_type=jnp.float32
    )
    gate_grad_tok = gate_flat.reshape(tokens_here, top_count).astype(jnp.bfloat16)
    return (acts_grad, gate_grad_tok, gate_grad[None], up_grad[None], down_grad[None])


def solution(mesh):
    planes = mesh.shape["ctx"]
    dense = mesh.shape["exp"] == 4 and mesh.shape["rep"] == 2
    placed = (
        P(("ctx", "exp"), "rep"),
        P(("ctx", "exp"), "rep"),
        P(("ctx", "exp"), None),
        P(("ctx", "exp"), None),
        P(("ctx", "exp"), "rep", None),
        P(("ctx", "exp"), "rep", None),
        P(("ctx", "exp"), "rep", None),
    )
    return jax.shard_map(
        functools.partial(dense_body, planes) if dense else sparse_body,
        mesh=mesh,
        in_specs=placed,
        out_specs=(
            P(("ctx", "exp"), "rep"),
            P(("ctx", "exp"), None),
            P(("ctx", "exp"), "rep", None),
            P(("ctx", "exp"), "rep", None),
            P(("ctx", "exp"), "rep", None),
        ),
        check_vma=False,
    )
```

```python
import functools
import heapq

import jax
import jax.numpy as jnp
from jax import lax
from jax.experimental import pallas as pl
from jax.experimental.pallas import tpu as pltpu
from jax.sharding import PartitionSpec as P

MESH = pl.DeviceIdType.MESH
LANES = 128
CONTRACT_LAST = (((1,), (1,)), ((), ()))
CONTRACT_FIRST = (((0,), (0,)), ((), ()))


def diag_planes(z, planes):
    low = z - (2 * z >= planes)
    return (low, low + 1)


def forwards(z, planes, array, source, rel):
    out = []
    if rel == 0:
        out += [("x", z, 1), ("y", z, 2)]
        if source <= z < planes - 1:
            out.append(("up", z + 1, 0))
        if source >= z > 0:
            out.append(("down", z - 1, 0))
    elif rel == 1:
        if array == 1 and source in diag_planes(z, planes):
            out.append(("y", z, 3))
    elif rel == 2:
        if array == 0 and source in diag_planes(z, planes):
            out.append(("x", z, 3))
    else:
        if source <= z < planes - 1 and source not in diag_planes(z + 1, planes):
            out.append(("up", z + 1, 3))
        if source >= z > 0 and source not in diag_planes(z - 1, planes):
            out.append(("down", z - 1, 3))
    return out


def arrival_order(planes):
    wire, hop = 1.4, 1.6
    order = [[] for _ in range(planes)]
    free = {}
    events = []
    count = 0
    for z in range(planes):
        for array in range(2):
            events.append((0.0, count, z, array, z, 0))
            count += 1
    heapq.heapify(events)
    while events:
        now, _, z, array, source, rel = heapq.heappop(events)
        order[z].append((array, source, rel))
        for link, to, rel_there in forwards(z, planes, array, source, rel):
            begin = max(now, free.get((z, link), 0.0))
            free[(z, link)] = begin + wire
            heapq.heappush(events, (begin + wire + hop, count, to, array, source, rel_there))
            count += 1
    return order


def at_xor(e, rel):
    x, y = e % 2, e // 2
    dx, dy = rel % 2, rel // 2
    new_x = x if dx == 0 else 1 - x
    new_y = y if dy == 0 else 1 - y
    return new_y * 2 + new_x


def position():
    return lax.axis_index("ctx"), lax.axis_index("exp"), lax.axis_index("rep")


def greet_all(planes):
    z, e, r = position()
    barrier = pltpu.get_barrier_semaphore()
    total = 0
    for dz in range(planes):
        for rel in range(4):
            for dr in range(2):
                if dz == 0 and rel == 0 and dr == 0:
                    continue
                pl.semaphore_signal(
                    barrier,
                    inc=1,
                    device_id={
                        "ctx": lax.rem(z + dz, planes),
                        "exp": at_xor(e, rel),
                        "rep": r if dr == 0 else 1 - r,
                    },
                    device_id_type=MESH,
                )
                total += 1
    pl.semaphore_wait(barrier, total)


LINKS = ("x", "y", "up", "down", "core")


def whole_wait(ref, sem):
    pltpu.make_async_copy(ref, ref, sem).wait()


def layer_kernel(
    planes, acts, grad, idx, prob, w_gate_in, w_up_in, w_down_in,
    acts_grad, gate_tok, gate_grad_out, up_grad_out, down_grad_out,
    acts_buf, grad_buf, gates, gates_all, gate_col,
    w_gate, w_up, w_down, gg_buf, gu_buf, gh_buf, gate_part, gate_in,
    terms_out, terms_own, core_buf, sum_buf, xy_buf, col_buf, z_buf,
    gate_grad, up_grad, down_grad,
    send_sem, recv_sem, swap_sem, gate_send, gate_recv, local_sem, weight_sem, result_sem,
    core_send, core_recv, xy_send, xy_recv, z_send, z_recv, g_send, g_recv,
):
    f32, bf16 = jnp.float32, jnp.bfloat16
    z, e, r = position()
    rows, width = acts.shape
    depth = 2 * width
    chips = planes * 4
    tokens = chips * rows
    plane_rows = 4 * rows
    top = idx.shape[0]
    hidden_here = w_gate.shape[0]

    loads = [
        pltpu.make_async_copy(src.at[0], dst, weight_sem.at[i])
        for i, (src, dst) in enumerate(((w_gate_in, w_gate), (w_up_in, w_up), (w_down_in, w_down)))
    ]
    for copy in loads:
        copy.start()
    idx_now, prob_now = idx[...], prob[...].astype(f32)
    for expert in range(chips):
        gates[expert, :, 0:rows] = jnp.sum(
            jnp.where(idx_now == expert, prob_now, 0.0), axis=0, keepdims=True
        )
        gates[expert, :, rows:LANES] = jnp.zeros((1, LANES - rows), f32)
    greet_all(planes)

    def others(with_core):
        for k in range(planes):
            for rel in range(4):
                for dr in range(2 if with_core else 1):
                    if k or rel or dr:
                        yield k, rel, dr

    def device(k, rel, dr):
        return {
            "ctx": lax.rem(z + k, planes),
            "exp": at_xor(e, rel),
            "rep": r if dr == 0 else 1 - r,
        }

    gate_copies = []
    for k, rel, _ in others(False):
        gate_copies.append(
            pltpu.make_async_remote_copy(
                src_ref=gates.at[lax.rem(z + k, planes) * 4 + at_xor(e, rel)],
                dst_ref=gates_all.at[z * 4 + rel],
                send_sem=gate_send.at[k, rel],
                recv_sem=gate_recv.at[k, rel],
                device_id=device(k, rel, 0),
                device_id_type=MESH,
            )
        )
    inputs, buffers = (acts, grad), (acts_buf, grad_buf)
    cols = pl.ds(pl.multiple_of(r * width, width), width)
    other_cols = pl.ds(pl.multiple_of((1 - r) * width, width), width)

    def chunk(array, source, rel, columns):
        return buffers[array].at[pl.ds((source * 4 + rel) * rows, rows), columns]

    mine = pl.ds(pl.multiple_of(z * plane_rows, plane_rows), rows)
    local = [
        pltpu.make_async_copy(inputs[a], buffers[a].at[mine, cols], local_sem.at[a]) for a in range(2)
    ]
    local.append(pltpu.make_async_copy(gates.at[z * 4 + e], gates_all.at[z * 4], local_sem.at[2]))

    def send(zi, array, source, rel, link, rel_there):
        target = {
            "x": {"ctx": z, "exp": at_xor(e, 1), "rep": r},
            "y": {"ctx": z, "exp": at_xor(e, 2), "rep": r},
            "up": {"ctx": z + 1, "exp": e, "rep": r},
            "down": {"ctx": z - 1, "exp": e, "rep": r},
            "core": {"ctx": z, "exp": e, "rep": 1 - r},
        }[link]
        own = source == zi and rel == 0
        sem = swap_sem if link == "core" else recv_sem
        return pltpu.make_async_remote_copy(
            src_ref=inputs[array] if own else chunk(array, source, rel, cols),
            dst_ref=chunk(array, source, rel_there, cols),
            send_sem=send_sem.at[LINKS.index(link), array, source, rel],
            recv_sem=sem.at[array, source, rel_there],
            device_id=target,
            device_id_type=MESH,
        )

    order = arrival_order(planes)
    for zi in range(planes):

        @pl.when(z == zi)
        def _():
            sent = []
            gates_out = False
            for array, source, rel in order[zi]:
                own = source == zi and rel == 0
                if not own:
                    if not gates_out:
                        for copy in gate_copies:
                            copy.start()
                        for copy in local:
                            copy.start()
                        gates_out = True
                    whole_wait(chunk(array, source, rel, cols), recv_sem.at[array, source, rel])
                steps = forwards(zi, planes, array, source, rel) + [("core", zi, rel)]
                for link, _, rel_there in steps:
                    copy = send(zi, array, source, rel, link, rel_there)
                    copy.start()
                    sent.append(copy)
            for copy in sent:
                copy.wait_send()

    for copy in local:
        copy.wait()
    for copy, (k, rel, _) in zip(gate_copies, others(False)):
        copy.wait_send()
        whole_wait(gates_all.at[lax.rem(z + planes - k, planes) * 4 + rel], gate_recv.at[k, rel])
    turned = jnp.transpose(jnp.concatenate([gates_all[s] for s in range(chips)], axis=0))
    for s in range(chips):
        gate_col[s * rows : (s + 1) * rows, :] = jnp.broadcast_to(turned[0:rows, s : s + 1], (rows, LANES))
    for copy in loads:
        copy.wait()
    for array in range(2):
        for source in range(planes):
            for rel in range(4):
                whole_wait(chunk(array, source, rel, other_cols), swap_sem.at[array, source, rel])

    partial = jnp.zeros((tokens, LANES), f32)
    for first in range(0, hidden_here, LANES):
        part = pl.ds(first, LANES)
        pre_gate = lax.dot_general(acts_buf[...], w_gate[part, :], CONTRACT_LAST, preferred_element_type=f32)
        pre_up = lax.dot_general(acts_buf[...], w_up[part, :], CONTRACT_LAST, preferred_element_type=f32)
        raw = lax.dot_general(grad_buf[...], w_down[part, :], CONTRACT_LAST, preferred_element_type=f32)
        sigma = jax.nn.sigmoid(pre_gate)
        swish = pre_gate * sigma
        hidden = (swish * pre_up).astype(bf16).astype(f32)
        partial = partial + hidden * raw
        hidden_grad = raw * gate_col[...]
        gg_buf[:, part] = (hidden_grad * pre_up * sigma * (1.0 + pre_gate * (1.0 - sigma))).astype(bf16)
        gu_buf[:, part] = (hidden_grad * swish).astype(bf16)
        gh_buf[:, part] = (hidden * gate_col[...]).astype(bf16)

    def terms(first, wide):
        part = pl.ds(pl.multiple_of(first, wide), wide)
        return jnp.dot(gg_buf[...], w_gate[:, part], preferred_element_type=f32) + jnp.dot(
            gu_buf[...], w_up[:, part], preferred_element_type=f32
        )

    wide = width // 2
    for first in range(0, width, wide):
        terms_out[:, pl.ds(first, wide)] = terms((1 - r) * width + first, wide).astype(bf16)
    after = list(range(1, planes)) + [0]
    core_copies = {}
    for k in after:
        place = pl.ds(pl.multiple_of(lax.rem(z + k, planes) * plane_rows, plane_rows), plane_rows)
        core_copies[k] = pltpu.make_async_remote_copy(
            src_ref=terms_out.at[place],
            dst_ref=core_buf.at[place],
            send_sem=core_send.at[k],
            recv_sem=core_recv.at[k],
            device_id=device(0, 0, 1),
            device_id_type=MESH,
        )
        core_copies[k].start()
    for first in range(0, width, wide):
        terms_own[:, pl.ds(first, wide)] = terms(r * width + first, wide)

    flat = jnp.sum(jnp.transpose(partial), axis=0, keepdims=True)
    for block in range(planes):
        gate_part[block] = flat[:, block * plane_rows : (block + 1) * plane_rows]

    xy_copies = {}
    for k in after:
        zz = lax.rem(z + k, planes)
        core_copies[k].wait_recv()
        for rel in (3, 1, 2, 0):
            block = pl.ds(pl.multiple_of((zz * 4 + rel) * rows, rows), rows)
            sum_buf[block, :] = (terms_own[block, :] + core_buf[block, :].astype(f32)).astype(bf16)
            if rel == 0:
                continue
            xy_copies[k, rel] = pltpu.make_async_remote_copy(
                src_ref=sum_buf.at[block],
                dst_ref=xy_buf.at[k, rel],
                send_sem=xy_send.at[k, rel],
                recv_sem=xy_recv.at[k, rel],
                device_id=device(0, rel, 0),
                device_id_type=MESH,
            )
            xy_copies[k, rel].start()
    part_copies = []
    slot = r * chips + z * 4
    for k, rel, dr in others(True):
        part_copies.append(
            pltpu.make_async_remote_copy(
                src_ref=gate_part.at[lax.rem(z + k, planes)],
                dst_ref=gate_in.at[slot + rel],
                send_sem=g_send.at[k, rel, dr],
                recv_sem=g_recv.at[k, rel, dr],
                device_id=device(k, rel, dr),
                device_id_type=MESH,
            )
        )
        part_copies[-1].start()
    own_part = pltpu.make_async_copy(gate_part.at[z], gate_in.at[slot], local_sem.at[3])
    own_part.start()

    def weight_grad(left, right, result, out, sem):
        for first in range(0, depth, 512):
            part = pl.ds(first, 512)
            result[:, part] = lax.dot_general(
                left[...], right[:, part], CONTRACT_FIRST, preferred_element_type=f32
            ).astype(bf16)
        copy = pltpu.make_async_copy(result, out.at[0], sem)
        copy.start()
        return copy

    results = [
        weight_grad(gg_buf, acts_buf, gate_grad, gate_grad_out, result_sem.at[0]),
        weight_grad(gu_buf, acts_buf, up_grad, up_grad_out, result_sem.at[1]),
    ]

    def column_total(k):
        block = pl.ds(pl.multiple_of((lax.rem(z + k, planes) * 4) * rows, rows), rows)
        total = sum_buf[block, :].astype(f32)
        for rel in (1, 2, 3):
            xy_copies[k, rel].wait_recv()
            total = total + xy_buf[k, rel].astype(f32)
        return total

    z_copies = {}
    for k in range(1, planes):
        col_buf[k] = column_total(k).astype(bf16)
        z_copies[k] = pltpu.make_async_remote_copy(
            src_ref=col_buf.at[k],
            dst_ref=z_buf.at[k],
            send_sem=z_send.at[k],
            recv_sem=z_recv.at[k],
            device_id=device(k, 0, 0),
            device_id_type=MESH,
        )
        z_copies[k].start()
    results.append(weight_grad(gh_buf, grad_buf, down_grad, down_grad_out, result_sem.at[2]))

    own_part.wait()
    for k, rel, dr in others(True):
        from_r = r if dr == 0 else 1 - r
        place = gate_in.at[from_r * chips + lax.rem(z + planes - k, planes) * 4 + rel]
        whole_wait(place, g_recv.at[k, rel, dr])
    token_grad = jnp.zeros((top, rows), f32)
    for s in range(chips):
        rel = s % 4
        row = (gate_in[s] + gate_in[chips + s]).astype(bf16).astype(f32)[:, rel * rows : (rel + 1) * rows]
        expert = (s // 4) * 4 + at_xor(e, rel)
        token_grad = token_grad + jnp.where(idx_now == expert, row, 0.0)
    gate_tok[...] = token_grad.astype(bf16)

    total = column_total(0)
    for k in range(1, planes):
        z_copies[k].wait_recv()
        total = total + z_buf[k].astype(f32)
    acts_grad[...] = total.astype(bf16)

    for copies in (core_copies, xy_copies, z_copies):
        for copy in copies.values():
            copy.wait_send()
    for copy in part_copies:
        copy.wait_send()
    for copy in results:
        copy.wait()


def dense_body(planes, acts, grad_out, experts_idx, gate_prob, w_gate, w_up, w_down):
    rows, width = acts.shape
    chips = planes * 4
    tokens = chips * rows
    depth = 2 * width
    hidden_here = w_gate.shape[1]
    dma = pltpu.SemaphoreType.DMA
    vmem, anywhere = pl.BlockSpec(memory_space=pltpu.VMEM), pl.BlockSpec(memory_space=pl.ANY)
    bf16, f32 = jnp.bfloat16, jnp.float32
    weight = pltpu.VMEM((hidden_here, depth), bf16)
    units = pltpu.VMEM((tokens, hidden_here), bf16)
    result = jax.ShapeDtypeStruct(w_gate.shape, bf16)
    block = (rows, width)

    acts_grad, gate_tok, gate_grad, up_grad, down_grad = pl.pallas_call(
        functools.partial(layer_kernel, planes),
        out_shape=(
            jax.ShapeDtypeStruct(block, bf16),
            jax.ShapeDtypeStruct(experts_idx.shape[::-1], bf16),
            result, result, result,
        ),
        in_specs=[vmem] * 4 + [anywhere] * 3,
        out_specs=[vmem] * 2 + [anywhere] * 3,
        scratch_shapes=[
            pltpu.VMEM((tokens, depth), bf16),
            pltpu.VMEM((tokens, depth), bf16),
            pltpu.VMEM((chips, 1, LANES), f32),
            pltpu.VMEM((chips, 1, LANES), f32),
            pltpu.VMEM((tokens, LANES), f32),
            weight, weight, weight,
            units, units, units,
            pltpu.VMEM((planes, 1, LANES), f32),
            pltpu.VMEM((2 * chips, 1, LANES), f32),
            pltpu.VMEM((tokens, width), bf16),
            pltpu.VMEM((tokens, width), f32),
            pltpu.VMEM((tokens, width), bf16),
            pltpu.VMEM((tokens, width), bf16),
            pltpu.VMEM((planes, 4, *block), bf16),
            pltpu.VMEM((planes, *block), bf16),
            pltpu.VMEM((planes, *block), bf16),
            weight, weight, weight,
            dma((len(LINKS), 2, planes, 4)),
            dma((2, planes, 4)),
            dma((2, planes, 4)),
            dma((planes, 4)),
            dma((planes, 4)),
            dma((4,)),
            dma((3,)),
            dma((3,)),
            dma((planes,)),
            dma((planes,)),
            dma((planes, 4)),
            dma((planes, 4)),
            dma((planes,)),
            dma((planes,)),
            dma((planes, 4, 2)),
            dma((planes, 4, 2)),
        ],
        compiler_params=pltpu.CompilerParams(
            collective_id=0, has_side_effects=True, vmem_limit_bytes=60 << 20
        ),
        name="layer",
    )(acts, grad_out, experts_idx.T, gate_prob.T, w_gate, w_up, w_down)
    return acts_grad, gate_tok.T, gate_grad, up_grad, down_grad


def body(planes, dense, acts, grad_out, experts_idx, *rest):
    run = functools.partial(dense_body, planes) if dense and 4 * acts.shape[0] == LANES else sparse_body
    return run(acts, grad_out, experts_idx, *rest)


def slot_tables(experts_idx, expert_count, capacity):
    tokens_here, top_count = experts_idx.shape
    labels = jnp.arange(expert_count, dtype=jnp.int32)
    picked = (experts_idx[:, :, None] == labels[None, None, :]).astype(jnp.int32)
    flat_pick = picked.reshape(tokens_here * top_count, expert_count)
    earlier = jnp.cumsum(flat_pick, axis=0) - flat_pick
    slot_number = jnp.sum(flat_pick * (labels[None, :] * capacity + earlier), axis=1)
    slot_labels = jnp.arange(expert_count * capacity, dtype=jnp.int32)
    select = (slot_number[None, :] == slot_labels[:, None]).astype(jnp.bfloat16)
    placing = jnp.sum(select.reshape(expert_count * capacity, tokens_here, top_count), axis=2)
    return (select, placing)


def sparse_body(acts, grad_out, experts_idx, gate_prob, w_gate, w_up, w_down):
    tokens_here, top_count = experts_idx.shape
    expert_count = lax.axis_size(("ctx", "exp"))
    capacity = min(tokens_here, 3 * tokens_here * top_count // (2 * expert_count))
    select, placing = slot_tables(experts_idx, expert_count, capacity)
    slot_gate = jnp.dot(select, gate_prob.reshape(-1), preferred_element_type=jnp.float32).astype(
        jnp.bfloat16
    )
    send_acts = jnp.dot(placing, acts, preferred_element_type=jnp.float32).astype(jnp.bfloat16)
    send_grad = jnp.dot(placing, grad_out, preferred_element_type=jnp.float32).astype(jnp.bfloat16)
    part_acts, part_grad, rows_gate = (
        lax.all_to_all(send_acts, ("ctx", "exp"), split_axis=0, concat_axis=0, tiled=True),
        lax.all_to_all(send_grad, ("ctx", "exp"), split_axis=0, concat_axis=0, tiled=True),
        lax.all_to_all(slot_gate, ("ctx", "exp"), split_axis=0, concat_axis=0, tiled=True),
    )
    rows_acts, rows_grad = (
        lax.all_gather(part_acts, "rep", axis=1, tiled=True),
        lax.all_gather(part_grad, "rep", axis=1, tiled=True),
    )
    gate_w = w_gate[0]
    up_w = w_up[0]
    down_w = w_down[0]
    contract_last = (((1,), (1,)), ((), ()))
    contract_first = (((0,), (0,)), ((), ()))
    pre_gate = lax.dot_general(rows_acts, gate_w, contract_last, preferred_element_type=jnp.float32)
    pre_up = lax.dot_general(rows_acts, up_w, contract_last, preferred_element_type=jnp.float32)
    sigma = jax.nn.sigmoid(pre_gate)
    swish = pre_gate * sigma
    hidden = (swish * pre_up).astype(jnp.bfloat16)
    expert_out = jnp.dot(hidden, down_w, preferred_element_type=jnp.float32)
    gate_part = jnp.sum(expert_out * rows_grad.astype(jnp.float32), axis=1)
    scaled_grad = (rows_gate.astype(jnp.float32)[:, None] * rows_grad.astype(jnp.float32)).astype(
        jnp.bfloat16
    )
    hidden_grad = lax.dot_general(
        scaled_grad, down_w, contract_last, preferred_element_type=jnp.float32
    )
    grad_gate_pre = (hidden_grad * pre_up * sigma * (1.0 + pre_gate * (1.0 - sigma))).astype(
        jnp.bfloat16
    )
    grad_up_pre = (hidden_grad * swish).astype(jnp.bfloat16)
    down_grad = lax.dot_general(
        hidden, scaled_grad, contract_first, preferred_element_type=jnp.float32
    ).astype(jnp.bfloat16)
    gate_grad = lax.dot_general(
        grad_gate_pre, rows_acts, contract_first, preferred_element_type=jnp.float32
    ).astype(jnp.bfloat16)
    up_grad = lax.dot_general(
        grad_up_pre, rows_acts, contract_first, preferred_element_type=jnp.float32
    ).astype(jnp.bfloat16)
    row_terms = jnp.dot(grad_gate_pre, gate_w, preferred_element_type=jnp.float32)
    row_terms = row_terms + jnp.dot(grad_up_pre, up_w, preferred_element_type=jnp.float32)
    row_share = lax.psum_scatter(
        row_terms.astype(jnp.bfloat16), "rep", scatter_dimension=1, tiled=True
    )
    gate_total = lax.psum(gate_part, "rep").astype(jnp.bfloat16)
    back_share, back_gate = (
        lax.all_to_all(row_share, ("ctx", "exp"), split_axis=0, concat_axis=0, tiled=True),
        lax.all_to_all(gate_total, ("ctx", "exp"), split_axis=0, concat_axis=0, tiled=True),
    )
    acts_grad = lax.dot_general(
        placing, back_share, contract_first, preferred_element_type=jnp.float32
    ).astype(jnp.bfloat16)
    gate_flat = lax.dot_general(
        select, back_gate, contract_first, preferred_element_type=jnp.float32
    )
    gate_grad_tok = gate_flat.reshape(tokens_here, top_count).astype(jnp.bfloat16)
    return (acts_grad, gate_grad_tok, gate_grad[None], up_grad[None], down_grad[None])


def solution(mesh):
    planes = mesh.shape["ctx"]
    dense = mesh.shape["exp"] == 4 and mesh.shape["rep"] == 2
    placed = (
        P(("ctx", "exp"), "rep"),
        P(("ctx", "exp"), "rep"),
        P(("ctx", "exp"), None),
        P(("ctx", "exp"), None),
        P(("ctx", "exp"), "rep", None),
        P(("ctx", "exp"), "rep", None),
        P(("ctx", "exp"), "rep", None),
    )
    return jax.shard_map(
        functools.partial(body, planes, dense),
        mesh=mesh,
        in_specs=placed,
        out_specs=(
            P(("ctx", "exp"), "rep"),
            P(("ctx", "exp"), None),
            P(("ctx", "exp"), "rep", None),
            P(("ctx", "exp"), "rep", None),
            P(("ctx", "exp"), "rep", None),
        ),
        check_vma=False,
    )
```

```python
import functools
import heapq

import jax
import jax.numpy as jnp
from jax import lax
from jax.experimental import pallas as pl
from jax.experimental.pallas import tpu as pltpu
from jax.sharding import PartitionSpec as P

MESH = pl.DeviceIdType.MESH
LANES = 128
CONTRACT_LAST = (((1,), (1,)), ((), ()))
CONTRACT_FIRST = (((0,), (0,)), ((), ()))


def diag_planes(z, planes):
    low = z - (2 * z >= planes)
    return (low, low + 1)


def forwards(z, planes, array, source, rel):
    out = []
    if rel == 0:
        out += [("x", z, 1), ("y", z, 2)]
        if source <= z < planes - 1:
            out.append(("up", z + 1, 0))
        if source >= z > 0:
            out.append(("down", z - 1, 0))
    elif rel == 1:
        if array == 1 and source in diag_planes(z, planes):
            out.append(("y", z, 3))
    elif rel == 2:
        if array == 0 and source in diag_planes(z, planes):
            out.append(("x", z, 3))
    else:
        if source <= z < planes - 1 and source not in diag_planes(z + 1, planes):
            out.append(("up", z + 1, 3))
        if source >= z > 0 and source not in diag_planes(z - 1, planes):
            out.append(("down", z - 1, 3))
    return out


def arrival_order(planes):
    wire, hop = 1.4, 1.6
    order = [[] for _ in range(planes)]
    free = {}
    events = []
    count = 0
    for z in range(planes):
        for array in range(2):
            events.append((0.0, count, z, array, z, 0))
            count += 1
    heapq.heapify(events)
    while events:
        now, _, z, array, source, rel = heapq.heappop(events)
        order[z].append((array, source, rel))
        for link, to, rel_there in forwards(z, planes, array, source, rel):
            begin = max(now, free.get((z, link), 0.0))
            free[(z, link)] = begin + wire
            heapq.heappush(events, (begin + wire + hop, count, to, array, source, rel_there))
            count += 1
    return order


def at_xor(e, rel):
    x, y = e % 2, e // 2
    dx, dy = rel % 2, rel // 2
    new_x = x if dx == 0 else 1 - x
    new_y = y if dy == 0 else 1 - y
    return new_y * 2 + new_x


def position():
    return lax.axis_index("ctx"), lax.axis_index("exp"), lax.axis_index("rep")


def greet_all(planes):
    z, e, r = position()
    barrier = pltpu.get_barrier_semaphore()
    total = 0
    for dz in range(planes):
        for rel in range(4):
            for dr in range(2):
                if dz == 0 and rel == 0 and dr == 0:
                    continue
                pl.semaphore_signal(
                    barrier,
                    inc=1,
                    device_id={
                        "ctx": lax.rem(z + dz, planes),
                        "exp": at_xor(e, rel),
                        "rep": r if dr == 0 else 1 - r,
                    },
                    device_id_type=MESH,
                )
                total += 1
    pl.semaphore_wait(barrier, total)


LINKS = ("x", "y", "up", "down", "core")


def whole_wait(ref, sem):
    pltpu.make_async_copy(ref, ref, sem).wait()


def layer_kernel(
    planes, acts, grad, idx_in, prob_in, w_gate_in, w_up_in, w_down_in,
    acts_grad, gate_tok, gate_grad_out, up_grad_out, down_grad_out,
    acts_buf, grad_buf, idx, prob, gates, gates_all, gate_col,
    w_gate, w_up, w_down, gg_buf, gu_buf, gh_buf, gate_part, gate_in,
    terms_out, terms_own, core_buf, sum_buf, xy_buf, col_buf, z_buf,
    gate_grad, up_grad, down_grad,
    send_sem, recv_sem, swap_sem, gate_send, gate_recv, local_sem, weight_sem, result_sem,
    core_send, core_recv, xy_send, xy_recv, z_send, z_recv, g_send, g_recv,
):
    f32, bf16 = jnp.float32, jnp.bfloat16
    z, e, r = position()
    rows, width = acts.shape
    depth = 2 * width
    chips = planes * 4
    tokens = chips * rows
    plane_rows = 4 * rows
    top = idx.shape[0]
    hidden_here = w_gate.shape[0]

    buffers = (acts_buf, grad_buf)
    cols = pl.ds(pl.multiple_of(r * width, width), width)
    other_cols = pl.ds(pl.multiple_of((1 - r) * width, width), width)
    mine = pl.ds(pl.multiple_of(z * plane_rows, plane_rows), rows)
    local = [
        pltpu.make_async_copy(src, dst, local_sem.at[i])
        for i, (src, dst) in enumerate((
            (idx_in, idx), (prob_in, prob),
            (acts, acts_buf.at[mine, cols]), (grad, grad_buf.at[mine, cols]),
        ))
    ]
    for copy in local:
        copy.start()
    loads = [
        pltpu.make_async_copy(src.at[0], dst, weight_sem.at[i])
        for i, (src, dst) in enumerate(((w_gate_in, w_gate), (w_up_in, w_up), (w_down_in, w_down)))
    ]
    for copy in loads:
        copy.start()
    for copy in local[:2]:
        copy.wait()
    idx_now, prob_now = idx[...], prob[...].astype(f32)
    for expert in range(chips):
        gates[expert, :, 0:rows] = jnp.sum(
            jnp.where(idx_now == expert, prob_now, 0.0), axis=0, keepdims=True
        )
        gates[expert, :, rows:LANES] = jnp.zeros((1, LANES - rows), f32)
    for copy in local[2:]:
        copy.wait()
    greet_all(planes)

    def others(with_core):
        for k in range(planes):
            for rel in range(4):
                for dr in range(2 if with_core else 1):
                    if k or rel or dr:
                        yield k, rel, dr

    def device(k, rel, dr):
        return {
            "ctx": lax.rem(z + k, planes),
            "exp": at_xor(e, rel),
            "rep": r if dr == 0 else 1 - r,
        }

    gate_copies = []
    for k, rel, _ in others(False):
        gate_copies.append(
            pltpu.make_async_remote_copy(
                src_ref=gates.at[lax.rem(z + k, planes) * 4 + at_xor(e, rel)],
                dst_ref=gates_all.at[z * 4 + rel],
                send_sem=gate_send.at[k, rel],
                recv_sem=gate_recv.at[k, rel],
                device_id=device(k, rel, 0),
                device_id_type=MESH,
            )
        )

    def chunk(array, source, rel, columns):
        return buffers[array].at[pl.ds((source * 4 + rel) * rows, rows), columns]

    own_gates = pltpu.make_async_copy(gates.at[z * 4 + e], gates_all.at[z * 4], local_sem.at[4])

    def send(zi, array, source, rel, link, rel_there):
        target = {
            "x": {"ctx": z, "exp": at_xor(e, 1), "rep": r},
            "y": {"ctx": z, "exp": at_xor(e, 2), "rep": r},
            "up": {"ctx": z + 1, "exp": e, "rep": r},
            "down": {"ctx": z - 1, "exp": e, "rep": r},
            "core": {"ctx": z, "exp": e, "rep": 1 - r},
        }[link]
        sem = swap_sem if link == "core" else recv_sem
        return pltpu.make_async_remote_copy(
            src_ref=chunk(array, source, rel, cols),
            dst_ref=chunk(array, source, rel_there, cols),
            send_sem=send_sem.at[LINKS.index(link), array, source, rel],
            recv_sem=sem.at[array, source, rel_there],
            device_id=target,
            device_id_type=MESH,
        )

    order = arrival_order(planes)
    for zi in range(planes):

        @pl.when(z == zi)
        def _():
            sent = []
            gates_out = False
            for array, source, rel in order[zi]:
                own = source == zi and rel == 0
                if not own:
                    if not gates_out:
                        for copy in gate_copies:
                            copy.start()
                        own_gates.start()
                        gates_out = True
                    whole_wait(chunk(array, source, rel, cols), recv_sem.at[array, source, rel])
                steps = forwards(zi, planes, array, source, rel) + [("core", zi, rel)]
                for link, _, rel_there in steps:
                    copy = send(zi, array, source, rel, link, rel_there)
                    copy.start()
                    sent.append(copy)
            for copy in sent:
                copy.wait_send()

    own_gates.wait()
    for copy, (k, rel, _) in zip(gate_copies, others(False)):
        copy.wait_send()
        whole_wait(gates_all.at[lax.rem(z + planes - k, planes) * 4 + rel], gate_recv.at[k, rel])
    turned = jnp.transpose(jnp.concatenate([gates_all[s] for s in range(chips)], axis=0))
    for s in range(chips):
        gate_col[s * rows : (s + 1) * rows, :] = jnp.broadcast_to(turned[0:rows, s : s + 1], (rows, LANES))
    for copy in loads:
        copy.wait()
    for array in range(2):
        for source in range(planes):
            for rel in range(4):
                whole_wait(chunk(array, source, rel, other_cols), swap_sem.at[array, source, rel])

    partial = jnp.zeros((tokens, LANES), f32)
    for first in range(0, hidden_here, LANES):
        part = pl.ds(first, LANES)
        pre_gate = lax.dot_general(acts_buf[...], w_gate[part, :], CONTRACT_LAST, preferred_element_type=f32)
        pre_up = lax.dot_general(acts_buf[...], w_up[part, :], CONTRACT_LAST, preferred_element_type=f32)
        raw = lax.dot_general(grad_buf[...], w_down[part, :], CONTRACT_LAST, preferred_element_type=f32)
        sigma = jax.nn.sigmoid(pre_gate)
        swish = pre_gate * sigma
        hidden = (swish * pre_up).astype(bf16).astype(f32)
        partial = partial + hidden * raw
        hidden_grad = raw * gate_col[...]
        gg_buf[:, part] = (hidden_grad * pre_up * sigma * (1.0 + pre_gate * (1.0 - sigma))).astype(bf16)
        gu_buf[:, part] = (hidden_grad * swish).astype(bf16)
        gh_buf[:, part] = (hidden * gate_col[...]).astype(bf16)

    def terms(first, wide):
        part = pl.ds(pl.multiple_of(first, wide), wide)
        return jnp.dot(gg_buf[...], w_gate[:, part], preferred_element_type=f32) + jnp.dot(
            gu_buf[...], w_up[:, part], preferred_element_type=f32
        )

    wide = width // 2
    for first in range(0, width, wide):
        terms_out[:, pl.ds(first, wide)] = terms((1 - r) * width + first, wide).astype(bf16)
    after = list(range(1, planes)) + [0]
    core_copies = {}
    for k in after:
        place = pl.ds(pl.multiple_of(lax.rem(z + k, planes) * plane_rows, plane_rows), plane_rows)
        core_copies[k] = pltpu.make_async_remote_copy(
            src_ref=terms_out.at[place],
            dst_ref=core_buf.at[place],
            send_sem=core_send.at[k],
            recv_sem=core_recv.at[k],
            device_id=device(0, 0, 1),
            device_id_type=MESH,
        )
        core_copies[k].start()
    for first in range(0, width, wide):
        terms_own[:, pl.ds(first, wide)] = terms(r * width + first, wide)

    flat = jnp.sum(jnp.transpose(partial), axis=0, keepdims=True)
    for block in range(planes):
        gate_part[block] = flat[:, block * plane_rows : (block + 1) * plane_rows]

    xy_copies = {}
    for k in after:
        zz = lax.rem(z + k, planes)
        core_copies[k].wait_recv()
        for rel in (3, 1, 2, 0):
            block = pl.ds(pl.multiple_of((zz * 4 + rel) * rows, rows), rows)
            sum_buf[block, :] = (terms_own[block, :] + core_buf[block, :].astype(f32)).astype(bf16)
            if rel == 0:
                continue
            xy_copies[k, rel] = pltpu.make_async_remote_copy(
                src_ref=sum_buf.at[block],
                dst_ref=xy_buf.at[k, rel],
                send_sem=xy_send.at[k, rel],
                recv_sem=xy_recv.at[k, rel],
                device_id=device(0, rel, 0),
                device_id_type=MESH,
            )
            xy_copies[k, rel].start()
    part_copies = []
    slot = r * chips + z * 4
    for k, rel, dr in others(True):
        part_copies.append(
            pltpu.make_async_remote_copy(
                src_ref=gate_part.at[lax.rem(z + k, planes)],
                dst_ref=gate_in.at[slot + rel],
                send_sem=g_send.at[k, rel, dr],
                recv_sem=g_recv.at[k, rel, dr],
                device_id=device(k, rel, dr),
                device_id_type=MESH,
            )
        )
        part_copies[-1].start()
    own_part = pltpu.make_async_copy(gate_part.at[z], gate_in.at[slot], local_sem.at[5])
    own_part.start()

    def weight_grad(left, right, result, out, sem):
        for first in range(0, depth, 512):
            part = pl.ds(first, 512)
            result[:, part] = lax.dot_general(
                left[...], right[:, part], CONTRACT_FIRST, preferred_element_type=f32
            ).astype(bf16)
        copy = pltpu.make_async_copy(result, out.at[0], sem)
        copy.start()
        return copy

    results = [
        weight_grad(gg_buf, acts_buf, gate_grad, gate_grad_out, result_sem.at[0]),
        weight_grad(gu_buf, acts_buf, up_grad, up_grad_out, result_sem.at[1]),
    ]

    def column_total(k):
        block = pl.ds(pl.multiple_of((lax.rem(z + k, planes) * 4) * rows, rows), rows)
        total = sum_buf[block, :].astype(f32)
        for rel in (1, 2, 3):
            xy_copies[k, rel].wait_recv()
            total = total + xy_buf[k, rel].astype(f32)
        return total

    z_copies = {}
    for k in range(1, planes):
        col_buf[k] = column_total(k).astype(bf16)
        z_copies[k] = pltpu.make_async_remote_copy(
            src_ref=col_buf.at[k],
            dst_ref=z_buf.at[k],
            send_sem=z_send.at[k],
            recv_sem=z_recv.at[k],
            device_id=device(k, 0, 0),
            device_id_type=MESH,
        )
        z_copies[k].start()
    results.append(weight_grad(gh_buf, grad_buf, down_grad, down_grad_out, result_sem.at[2]))

    own_part.wait()
    for k, rel, dr in others(True):
        from_r = r if dr == 0 else 1 - r
        place = gate_in.at[from_r * chips + lax.rem(z + planes - k, planes) * 4 + rel]
        whole_wait(place, g_recv.at[k, rel, dr])
    token_grad = jnp.zeros((top, rows), f32)
    for s in range(chips):
        rel = s % 4
        row = (gate_in[s] + gate_in[chips + s]).astype(bf16).astype(f32)[:, rel * rows : (rel + 1) * rows]
        expert = (s // 4) * 4 + at_xor(e, rel)
        token_grad = token_grad + jnp.where(idx_now == expert, row, 0.0)
    gate_tok[...] = token_grad.astype(bf16)

    total = column_total(0)
    for k in range(1, planes):
        z_copies[k].wait_recv()
        total = total + z_buf[k].astype(f32)
    acts_grad[...] = total.astype(bf16)

    for copies in (core_copies, xy_copies, z_copies):
        for copy in copies.values():
            copy.wait_send()
    for copy in part_copies:
        copy.wait_send()
    for copy in results:
        copy.wait()


def finish_kernel(*refs):
    count = len(refs) // 2
    sem = refs[-1]
    copies = [pltpu.make_async_copy(refs[i], refs[count + i], sem.at[i]) for i in range(count)]
    for copy in copies:
        copy.start()
    for copy in copies:
        copy.wait()


def dense_body(planes, acts, grad_out, experts_idx, gate_prob, w_gate, w_up, w_down):
    rows, width = acts.shape
    chips = planes * 4
    tokens = chips * rows
    depth = 2 * width
    hidden_here = w_gate.shape[1]
    dma = pltpu.SemaphoreType.DMA
    vmem, anywhere = pl.BlockSpec(memory_space=pltpu.VMEM), pl.BlockSpec(memory_space=pl.ANY)
    bf16, f32 = jnp.bfloat16, jnp.float32
    weight = pltpu.VMEM((hidden_here, depth), bf16)
    units = pltpu.VMEM((tokens, hidden_here), bf16)
    result = jax.ShapeDtypeStruct(w_gate.shape, bf16)
    block = (rows, width)

    shapes = (
        jax.ShapeDtypeStruct(block, bf16),
        jax.ShapeDtypeStruct(experts_idx.shape[::-1], bf16),
        result, result, result,
    )
    results = pl.pallas_call(
        functools.partial(layer_kernel, planes),
        out_shape=shapes,
        in_specs=[pl.BlockSpec(memory_space=pltpu.HBM)] * 7,
        out_specs=[vmem] * 2 + [anywhere] * 3,
        scratch_shapes=[
            pltpu.VMEM((tokens, depth), bf16),
            pltpu.VMEM((tokens, depth), bf16),
            pltpu.VMEM(experts_idx.shape[::-1], jnp.int32),
            pltpu.VMEM(gate_prob.shape[::-1], bf16),
            pltpu.VMEM((chips, 1, LANES), f32),
            pltpu.VMEM((chips, 1, LANES), f32),
            pltpu.VMEM((tokens, LANES), f32),
            weight, weight, weight,
            units, units, units,
            pltpu.VMEM((planes, 1, LANES), f32),
            pltpu.VMEM((2 * chips, 1, LANES), f32),
            pltpu.VMEM((tokens, width), bf16),
            pltpu.VMEM((tokens, width), f32),
            pltpu.VMEM((tokens, width), bf16),
            pltpu.VMEM((tokens, width), bf16),
            pltpu.VMEM((planes, 4, *block), bf16),
            pltpu.VMEM((planes, *block), bf16),
            pltpu.VMEM((planes, *block), bf16),
            weight, weight, weight,
            dma((len(LINKS), 2, planes, 4)),
            dma((2, planes, 4)),
            dma((2, planes, 4)),
            dma((planes, 4)),
            dma((planes, 4)),
            dma((6,)),
            dma((3,)),
            dma((3,)),
            dma((planes,)),
            dma((planes,)),
            dma((planes, 4)),
            dma((planes, 4)),
            dma((planes,)),
            dma((planes,)),
            dma((planes, 4, 2)),
            dma((planes, 4, 2)),
        ],
        compiler_params=pltpu.CompilerParams(
            collective_id=0, has_side_effects=True, vmem_limit_bytes=34 << 20
        ),
        name="layer",
    )(*(
        pltpu.with_memory_space_constraint(array, pltpu.HBM)
        for array in (acts, grad_out, experts_idx.T, gate_prob.T, w_gate, w_up, w_down)
    ))
    acts_grad, gate_tok, gate_grad, up_grad, down_grad = pl.pallas_call(
        finish_kernel,
        out_shape=shapes,
        in_specs=[vmem] * len(shapes),
        out_specs=[anywhere] * len(shapes),
        scratch_shapes=[dma((len(shapes),))],
        compiler_params=pltpu.CompilerParams(vmem_limit_bytes=16 << 20),
        name="finish",
    )(*results)
    return acts_grad, gate_tok.T, gate_grad, up_grad, down_grad


def body(planes, dense, acts, grad_out, experts_idx, *rest):
    run = functools.partial(dense_body, planes) if dense and 4 * acts.shape[0] == LANES else sparse_body
    return run(acts, grad_out, experts_idx, *rest)


def slot_tables(experts_idx, expert_count, capacity):
    tokens_here, top_count = experts_idx.shape
    labels = jnp.arange(expert_count, dtype=jnp.int32)
    picked = (experts_idx[:, :, None] == labels[None, None, :]).astype(jnp.int32)
    flat_pick = picked.reshape(tokens_here * top_count, expert_count)
    earlier = jnp.cumsum(flat_pick, axis=0) - flat_pick
    slot_number = jnp.sum(flat_pick * (labels[None, :] * capacity + earlier), axis=1)
    slot_labels = jnp.arange(expert_count * capacity, dtype=jnp.int32)
    select = (slot_number[None, :] == slot_labels[:, None]).astype(jnp.bfloat16)
    placing = jnp.sum(select.reshape(expert_count * capacity, tokens_here, top_count), axis=2)
    return (select, placing)


def sparse_body(acts, grad_out, experts_idx, gate_prob, w_gate, w_up, w_down):
    tokens_here, top_count = experts_idx.shape
    expert_count = lax.axis_size(("ctx", "exp"))
    capacity = min(tokens_here, 3 * tokens_here * top_count // (2 * expert_count))
    select, placing = slot_tables(experts_idx, expert_count, capacity)
    slot_gate = jnp.dot(select, gate_prob.reshape(-1), preferred_element_type=jnp.float32).astype(
        jnp.bfloat16
    )
    send_acts = jnp.dot(placing, acts, preferred_element_type=jnp.float32).astype(jnp.bfloat16)
    send_grad = jnp.dot(placing, grad_out, preferred_element_type=jnp.float32).astype(jnp.bfloat16)
    part_acts, part_grad, rows_gate = (
        lax.all_to_all(send_acts, ("ctx", "exp"), split_axis=0, concat_axis=0, tiled=True),
        lax.all_to_all(send_grad, ("ctx", "exp"), split_axis=0, concat_axis=0, tiled=True),
        lax.all_to_all(slot_gate, ("ctx", "exp"), split_axis=0, concat_axis=0, tiled=True),
    )
    rows_acts, rows_grad = (
        lax.all_gather(part_acts, "rep", axis=1, tiled=True),
        lax.all_gather(part_grad, "rep", axis=1, tiled=True),
    )
    gate_w = w_gate[0]
    up_w = w_up[0]
    down_w = w_down[0]
    contract_last = (((1,), (1,)), ((), ()))
    contract_first = (((0,), (0,)), ((), ()))
    pre_gate = lax.dot_general(rows_acts, gate_w, contract_last, preferred_element_type=jnp.float32)
    pre_up = lax.dot_general(rows_acts, up_w, contract_last, preferred_element_type=jnp.float32)
    sigma = jax.nn.sigmoid(pre_gate)
    swish = pre_gate * sigma
    hidden = (swish * pre_up).astype(jnp.bfloat16)
    expert_out = jnp.dot(hidden, down_w, preferred_element_type=jnp.float32)
    gate_part = jnp.sum(expert_out * rows_grad.astype(jnp.float32), axis=1)
    scaled_grad = (rows_gate.astype(jnp.float32)[:, None] * rows_grad.astype(jnp.float32)).astype(
        jnp.bfloat16
    )
    hidden_grad = lax.dot_general(
        scaled_grad, down_w, contract_last, preferred_element_type=jnp.float32
    )
    grad_gate_pre = (hidden_grad * pre_up * sigma * (1.0 + pre_gate * (1.0 - sigma))).astype(
        jnp.bfloat16
    )
    grad_up_pre = (hidden_grad * swish).astype(jnp.bfloat16)
    down_grad = lax.dot_general(
        hidden, scaled_grad, contract_first, preferred_element_type=jnp.float32
    ).astype(jnp.bfloat16)
    gate_grad = lax.dot_general(
        grad_gate_pre, rows_acts, contract_first, preferred_element_type=jnp.float32
    ).astype(jnp.bfloat16)
    up_grad = lax.dot_general(
        grad_up_pre, rows_acts, contract_first, preferred_element_type=jnp.float32
    ).astype(jnp.bfloat16)
    row_terms = jnp.dot(grad_gate_pre, gate_w, preferred_element_type=jnp.float32)
    row_terms = row_terms + jnp.dot(grad_up_pre, up_w, preferred_element_type=jnp.float32)
    row_share = lax.psum_scatter(
        row_terms.astype(jnp.bfloat16), "rep", scatter_dimension=1, tiled=True
    )
    gate_total = lax.psum(gate_part, "rep").astype(jnp.bfloat16)
    back_share, back_gate = (
        lax.all_to_all(row_share, ("ctx", "exp"), split_axis=0, concat_axis=0, tiled=True),
        lax.all_to_all(gate_total, ("ctx", "exp"), split_axis=0, concat_axis=0, tiled=True),
    )
    acts_grad = lax.dot_general(
        placing, back_share, contract_first, preferred_element_type=jnp.float32
    ).astype(jnp.bfloat16)
    gate_flat = lax.dot_general(
        select, back_gate, contract_first, preferred_element_type=jnp.float32
    )
    gate_grad_tok = gate_flat.reshape(tokens_here, top_count).astype(jnp.bfloat16)
    return (acts_grad, gate_grad_tok, gate_grad[None], up_grad[None], down_grad[None])


def solution(mesh):
    planes = mesh.shape["ctx"]
    dense = mesh.shape["exp"] == 4 and mesh.shape["rep"] == 2
    placed = (
        P(("ctx", "exp"), "rep"),
        P(("ctx", "exp"), "rep"),
        P(("ctx", "exp"), None),
        P(("ctx", "exp"), None),
        P(("ctx", "exp"), "rep", None),
        P(("ctx", "exp"), "rep", None),
        P(("ctx", "exp"), "rep", None),
    )
    return jax.shard_map(
        functools.partial(body, planes, dense),
        mesh=mesh,
        in_specs=placed,
        out_specs=(
            P(("ctx", "exp"), "rep"),
            P(("ctx", "exp"), None),
            P(("ctx", "exp"), "rep", None),
            P(("ctx", "exp"), "rep", None),
            P(("ctx", "exp"), "rep", None),
        ),
        check_vma=False,
    )
```
